32 devices in a mesh: batch: 8 (over y, x, core), wide: 4 (over z).
Axes of the slice: x: 2, y: 2, z: 4, core: 2. Of those that a mesh axis runs over, the one named last changes fastest.
Arguments:
- tokens: bfloat16 [16384, 1024], P(('batch', 'wide')), may hold values from -6 to 6
- ln_gain: float32 [1024], replicated, may hold values from 0.1 to 1.9
- w_qkv: bfloat16 [1024, 3072], P(None, 'wide'), may hold values from -0.1875 to 0.1875
- q_gain: float32 [64], replicated, may hold values from 0.1 to 1.9
- k_gain: float32 [64], replicated, may hold values from 0.1 to 1.9
- w_up: bfloat16 [1024, 4096], P(None, 'wide'), may hold values from -0.1875 to 0.1875
- w_out_attn: bfloat16 [1024, 1024], P('wide'), may hold values from -1.5 to 1.5
- w_down: bfloat16 [4096, 1024], P('wide'), may hold values from -0.09375 to 0.09375
- cotangent: bfloat16 [16384, 1024], P(('batch', 'wide')), may hold values from -6 to 6
- lengths: int32 [16], P('batch'), may hold values from 196 to 1024, as said below
Outputs:
- output: bfloat16 [16384, 1024], P(('batch', 'wide'))
- input_grad: float32 [16384, 1024], P(('batch', 'wide'))
- ln_gain_grad: float32 [1024], replicated
- w_qkv_grad: float32 [1024, 3072], P(None, 'wide')
- q_gain_grad: float32 [64], replicated
- k_gain_grad: float32 [64], replicated
- w_up_grad: float32 [1024, 4096], P(None, 'wide')
- w_out_attn_grad: float32 [1024, 1024], P('wide')
- w_down_grad: float32 [4096, 1024], P('wide')
The draws below stay inside these ranges and needn't reach their ends.
Inputs may be any that keep to these rules, and one draw needn't show every extreme that they name: `lengths`: every entry is 1024, 576 or 196.
All inputs are finite; a program needn't handle non-finite values.
Results may differ from the reference program's by a relative error of at most 0.013.
Values may be sent and summed in bfloat16 or wider, within the bound.
No kernel may reach another device: no remote copies, remote signals or barrier semaphores. Data moves between devices by JAX's collectives and lax.ppermute only.
A program may use at most 192 MiB of HBM per device.

```python
import math
import jax
import jax.numpy as jnp
from jax import lax

D = 1024
HEADS = 16
HEAD = 64
FF = 4096
SLOTS = 1024
IMAGES = 16
TOKENS = 16384


def draw_lengths(key, part):
    classes = jax.random.randint(key, (IMAGES,), 0, 6)
    medium = 9 * SLOTS // 16
    smallest = 49 * SLOTS // 256
    picked = jnp.where(classes < 3, SLOTS, jnp.where(classes < 5, medium, smallest))
    position = jnp.arange(IMAGES)
    picked = jnp.where(position == 0, SLOTS, picked)
    picked = jnp.where(position == 1, smallest, picked)
    return picked.astype(jnp.int32)


def block_levels(own_key, extent, split, low, largest):
    loudness = 1.0
    for dim, parts in split:
        draws = jax.random.uniform(jax.random.fold_in(jax.random.fold_in(own_key, 6), dim), (parts,), jnp.float32, low / len(split), largest / len(split))
        loudness = loudness * jnp.repeat(jnp.exp(draws), extent[dim] // parts).reshape((-1,) + (1,) * (len(extent) - 1 - dim))
    return loudness


def gaussian(stream_key, extent, width, bound, split=(), held_as=jnp.bfloat16):
    loudness = block_levels(stream_key, extent, split, -0.22, 0.18) if split else 1.0
    array = jax.random.normal(stream_key, extent, jnp.float32) * width * loudness
    return jnp.minimum(jnp.maximum(array, -bound), bound).astype(held_as)


def setup_inputs(seed: int = 0) -> dict:
    key_of = jax.random.split(jax.random.key(seed), 11)
    tokens = gaussian(key_of[0], (TOKENS, D), 1.0, 6.0, ((0, 32),))
    ln_gain = jnp.clip(1.0 + 0.18 * jax.random.normal(key_of[1], (D,), jnp.float32), 0.1, 1.9)
    w_qkv = gaussian(key_of[2], (D, 3 * D), D ** -0.5, 0.1875, ((1, 4),))
    q_gain = jnp.clip(1.0 + 0.18 * jax.random.normal(key_of[3], (HEAD,), jnp.float32), 0.1, 1.9)
    k_gain = jnp.clip(1.0 + 0.18 * jax.random.normal(key_of[4], (HEAD,), jnp.float32), 0.1, 1.9)
    w_up = gaussian(key_of[5], (D, FF), D ** -0.5, 0.1875, ((1, 4),))
    w_out_attn = gaussian(key_of[6], (D, D), (HEAD // 4) ** -0.5, 1.5, ((0, 4),))
    w_down = gaussian(key_of[7], (FF, D), FF ** -0.5, 0.09375, ((0, 4),))
    cotangent = gaussian(key_of[8], (TOKENS, D), 1.0, 6.0, ((0, 32),))
    lengths = draw_lengths(jax.random.fold_in(key_of[10], 71), 0)
    return {"tokens": tokens, "ln_gain": ln_gain, "w_qkv": w_qkv, "q_gain": q_gain, "k_gain": k_gain, "w_up": w_up, "w_out_attn": w_out_attn, "w_down": w_down, "cotangent": cotangent, "lengths": lengths}


@jax.custom_vjp
def low(v):
    return lax.optimization_barrier(v.astype(jnp.bfloat16)).astype(jnp.float32)

@jax.custom_vjp
def low_back(v):
    return v

def low_keep(v):
    return (low(v), None)

def low_pass(kept, grad):
    return (grad,)

def back_keep(v):
    return (v, None)

def back_low(kept, grad):
    return (low(grad),)
low.defvjp(low_keep, low_pass)
low_back.defvjp(back_keep, back_low)

def normalize(field):
    row_mean = lax.optimization_barrier(jnp.mean(field, axis=-1, keepdims=True))
    centred = field - row_mean
    variance = lax.optimization_barrier(jnp.mean(centred * centred, axis=-1, keepdims=True))
    return centred * lax.rsqrt(variance + 1e-06)

def image_attention(inputs):
    queries, keys_low, values, length = inputs
    score_scale = 1.0 / math.sqrt(HEAD)
    scores = jnp.einsum('qhd,khd->hqk', queries, keys_low, precision=lax.Precision.HIGHEST) * score_scale
    scores = low_back(scores)
    valid_keys = jnp.arange(SLOTS) < length
    scores = jnp.where(valid_keys[None, None, :], scores, -1e+30)
    probs = low(jax.nn.softmax(scores, axis=-1))
    return jnp.einsum('hqk,khd->qhd', probs, values, precision=lax.Precision.HIGHEST)

def forward(tokens, ln_gain, w_qkv, q_gain, k_gain, w_up, w_out_attn, w_down, lengths):
    row_count = tokens.shape[0]
    normed = low(normalize(tokens) * ln_gain)
    raw_proj = low_back(jnp.dot(normed, w_qkv, precision=lax.Precision.HIGHEST))
    raw_proj = raw_proj.reshape(row_count, HEADS, 3, HEAD)
    queries = low(normalize(raw_proj[:, :, 0]) * q_gain)
    keys_low = low(normalize(raw_proj[:, :, 1]) * k_gain)
    values = low(raw_proj[:, :, 2])
    image_shape = (row_count // SLOTS, SLOTS, HEADS, HEAD)
    attended = lax.map(jax.checkpoint(image_attention), (queries.reshape(image_shape), keys_low.reshape(image_shape), values.reshape(image_shape), lengths))
    attended = low(low_back(attended.reshape(row_count, D)))
    up_proj = low_back(jnp.dot(normed, w_up, precision=lax.Precision.HIGHEST))
    hidden = low(jax.nn.gelu(up_proj, approximate=False))
    branch = jnp.dot(attended, w_out_attn, precision=lax.Precision.HIGHEST) + jnp.dot(hidden, w_down, precision=lax.Precision.HIGHEST)
    return tokens + branch

def reference(tokens, ln_gain, w_qkv, q_gain, k_gain, w_up, w_out_attn, w_down, cotangent, lengths):
    floats = (tokens.astype(jnp.float32), ln_gain.astype(jnp.float32), w_qkv.astype(jnp.float32), q_gain.astype(jnp.float32), k_gain.astype(jnp.float32), w_up.astype(jnp.float32), w_out_attn.astype(jnp.float32), w_down.astype(jnp.float32))

    def closed(tok_in, gain_in, qkv_in, qg_in, kg_in, up_in, out_in, down_in):
        return forward(tok_in, gain_in, qkv_in, qg_in, kg_in, up_in, out_in, down_in, lengths)
    result, pullback = jax.vjp(closed, *floats)
    grads = pullback(cotangent.astype(jnp.float32))
    return (result.astype(jnp.bfloat16), grads[0], grads[1], grads[2], grads[3], grads[4], grads[5], grads[6], grads[7])
```

```python
from functools import partial
import math

import jax
import jax.numpy as jnp
from jax import lax
from jax.experimental import pallas as pl
from jax.experimental.pallas import tpu as pltpu
from jax.sharding import PartitionSpec as P

F32 = jnp.float32
LOW = jnp.bfloat16
LOG2E = math.log2(math.e)
LN2 = math.log(2.0)


def nn(a, b):
    return lax.dot_general(a, b, (((1,), (0,)), ((), ())), preferred_element_type=F32)


def nt(a, b):
    return lax.dot_general(a, b, (((1,), (1,)), ((), ())), preferred_element_type=F32)


def tn(a, b):
    return lax.dot_general(a, b, (((0,), (0,)), ((), ())), preferred_element_type=F32)


def normalize(field):
    row_mean = jnp.mean(field, axis=-1, keepdims=True)
    centred = field - row_mean
    variance = jnp.mean(centred * centred, axis=-1, keepdims=True)
    inv = lax.rsqrt(variance + 1e-06)
    return centred * inv, inv


def project_kernel(x_ref, w_ref, gains_ref, q_ref, k_ref, v_ref, rstd_ref, *, size):
    raw = nt(w_ref[...], x_ref[...])

    def norm(part):
        centred = part - jnp.mean(part, axis=0, keepdims=True)
        inv = lax.rsqrt(jnp.mean(centred * centred, axis=0, keepdims=True) + 1e-06)
        return centred * inv, inv

    query, query_inv = norm(raw[:size])
    key, key_inv = norm(raw[size : 2 * size])
    q_ref[...] = (query * gains_ref[:, 0:1]).astype(LOW)
    k_ref[...] = (key * gains_ref[:, 1:2]).astype(LOW)
    v_ref[...] = raw[2 * size :].astype(LOW)
    rstd_ref[0, 0:1, :] = query_inv
    rstd_ref[0, 1:2, :] = key_inv


def project(x, w_t, gains, size):
    heads = w_t.shape[0] // (3 * size)
    rows, width = x.shape
    out = pl.BlockSpec((size, rows), lambda h: (h, 0))
    shape = jax.ShapeDtypeStruct((heads * size, rows), LOW)
    return pl.pallas_call(
        partial(project_kernel, size=size),
        grid=(heads,),
        in_specs=[
            pl.BlockSpec((rows, width), lambda h: (0, 0)),
            pl.BlockSpec((3 * size, width), lambda h: (h, 0)),
            pl.BlockSpec((size, 2), lambda h: (0, 0)),
        ],
        out_specs=[out, out, out, pl.BlockSpec((1, 2, rows), lambda h: (h, 0, 0))],
        out_shape=[shape, shape, shape, jax.ShapeDtypeStruct((heads, 2, rows), F32)],
        compiler_params=pltpu.CompilerParams(vmem_limit_bytes=56 << 20),
        name="project",
    )(x, w_t, gains)


def attend_kernel(
    q_ref, k_ref, v_ref, g_ref, bias_ref, rstd_ref, gains_ref,
    att_ref, raw_ref, gain_ref, dq_ref, *, tile, size, score_scale
):
    slots = k_ref.shape[1]
    k_t = k_ref[...]
    v_t = v_ref[...]
    k_n = k_t.astype(F32).T.astype(LOW)
    v_n = v_t.astype(F32).T
    v_aug = jnp.concatenate([v_n, jnp.ones((slots, size), F32)], axis=1).astype(LOW)
    bias = bias_ref[...]
    dk = jnp.zeros((size, slots), F32)
    dv = jnp.zeros((size, slots), F32)
    for step in range(slots // tile):
        here = slice(step * tile, (step + 1) * tile)
        q_t = q_ref[:, here]
        q_n = q_t.astype(F32).T.astype(LOW)
        g_n = g_ref[:, here].astype(F32).T
        weights = jnp.exp2(nn(q_n, k_t) + bias)
        weights_low = weights.astype(LOW)
        summed = nn(weights_low, v_aug)
        inv = 1.0 / summed[:, size : size + 1]
        att = summed[:, :size] * inv
        g_scaled = g_n * inv
        inner = jnp.sum(g_scaled * att, axis=1, keepdims=True)
        dp = nn(g_scaled.astype(LOW), v_t)
        ds = (weights * (dp - inner)).astype(LOW)
        att_ref[:, here] = att.T.astype(LOW)
        dv = dv + nn(g_scaled.T.astype(LOW), weights_low)
        dk = dk + nn(q_t, ds)
        dq_ref[:, here] = nn(ds, k_n).T

    def norm_back(grad, scaled, gain, fold, inv):
        n = scaled.astype(F32) * (1.0 / (gain * fold))
        u = grad * gain
        back = inv * (
            u - jnp.mean(u, axis=0, keepdims=True) - n * jnp.mean(u * n, axis=0, keepdims=True)
        )
        product = grad * n
        lanes = sum(product[:, c : c + 128] for c in range(0, slots, 128))
        return back, lanes

    q_back, q_lanes = norm_back(
        dq_ref[...] * score_scale, q_ref[...], gains_ref[:, 0:1], LOG2E * score_scale, rstd_ref[0, 0:1, :]
    )
    k_back, k_lanes = norm_back(dk * LN2, k_t, gains_ref[:, 1:2], 1.0, rstd_ref[0, 1:2, :])
    raw_ref[:size, :] = q_back.astype(LOW)
    raw_ref[size : 2 * size, :] = k_back.astype(LOW)
    raw_ref[2 * size :, :] = dv.astype(LOW)

    @pl.when(pl.program_id(0) == 0)
    def _():
        gain_ref[...] = jnp.zeros_like(gain_ref)

    gain_ref[:size, :] += q_lanes
    gain_ref[size:, :] += k_lanes


def attend(q_t, k_t, v_t, g_t, bias, rstd, gains, size, score_scale):
    features, slots = q_t.shape
    heads = features // size
    head = pl.BlockSpec((size, slots), lambda h: (h, 0))
    return pl.pallas_call(
        partial(attend_kernel, tile=min(512, slots), size=size, score_scale=score_scale),
        grid=(heads,),
        in_specs=[
            head, head, head, head,
            pl.BlockSpec((1, slots), lambda h: (0, 0)),
            pl.BlockSpec((1, 2, slots), lambda h: (h, 0, 0)),
            pl.BlockSpec((size, 2), lambda h: (0, 0)),
        ],
        out_specs=[
            head,
            pl.BlockSpec((3 * size, slots), lambda h: (h, 0)),
            pl.BlockSpec((2 * size, 128), lambda h: (0, 0)),
        ],
        out_shape=[
            jax.ShapeDtypeStruct((features, slots), LOW),
            jax.ShapeDtypeStruct((3 * features, slots), LOW),
            jax.ShapeDtypeStruct((2 * size, 128), F32),
        ],
        scratch_shapes=[pltpu.VMEM((size, slots), F32)],
        compiler_params=pltpu.CompilerParams(vmem_limit_bytes=56 << 20),
        name="attend",
    )(q_t, k_t, v_t, g_t, bias, rstd, gains)


def feed_kernel(x_ref, c_ref, up_ref, down_ref, hidden_ref, grad_ref):
    up = nt(up_ref[...], x_ref[...])
    grad_hidden = nt(down_ref[...], c_ref[...])
    half = 0.5 + 0.5 * lax.erf(up * math.sqrt(0.5))
    bell = jnp.exp(up * up * -0.5) * (1.0 / math.sqrt(2.0 * math.pi))
    hidden_ref[...] = (up * half).astype(LOW)
    grad_ref[...] = (grad_hidden * (half + up * bell)).astype(LOW)


def feed(x, cot, w_up_t, w_down):
    units, width = w_up_t.shape
    rows = x.shape[0]
    tile = min(256, units)
    whole = pl.BlockSpec((rows, width), lambda i: (0, 0))
    part = pl.BlockSpec((tile, width), lambda i: (i, 0))
    out = pl.BlockSpec((tile, rows), lambda i: (i, 0))
    shape = jax.ShapeDtypeStruct((units, rows), LOW)
    return pl.pallas_call(
        feed_kernel,
        grid=(units // tile,),
        in_specs=[whole, whole, part, part],
        out_specs=[out, out],
        out_shape=[shape, shape],
        compiler_params=pltpu.CompilerParams(vmem_limit_bytes=56 << 20),
        name="feed",
    )(x, cot, w_up_t, w_down)


def pick(array, index, axis):
    return lax.dynamic_index_in_dim(array, index, axis, keepdims=False)


class Group:
    def __init__(self, size):
        self.size = size
        self.bits = size.bit_length() - 1
        index = lax.axis_index("batch")
        self.index = index
        self.bit = [(index >> i) & 1 for i in range(self.bits)]
        others = list(range(1, self.bits))
        self.orders = [others, others[::-1]]

    def swap(self, array, bit):
        return lax.ppermute(array, "batch", [(b, b ^ (1 << bit)) for b in range(self.size)])

    def halve(self, array, bit, live):
        axis = live.index(bit)
        kept = pick(array, self.bit[bit], axis)
        sent = pick(array, 1 - self.bit[bit], axis)
        got = self.swap(sent, bit)
        return (kept.astype(F32) + got.astype(F32)).astype(LOW), [b for b in live if b != bit]

    def double(self, array, bit, live):
        got = self.swap(array, bit)
        live = sorted(live + [bit], reverse=True)
        axis = live.index(bit)
        mine, theirs = jnp.expand_dims(array, axis), jnp.expand_dims(got, axis)
        low = self.bit[bit] == 0
        return jnp.concatenate(
            [jnp.where(low, mine, theirs), jnp.where(low, theirs, mine)], axis=axis
        ), live

    def scatter(self, array):
        rows, width = array.shape[1:]
        live = list(range(self.bits))[::-1]
        array = array.reshape([2] * self.bits + [rows, width])
        array, live = self.halve(array, 0, live)
        parts = []
        for part, order in zip(jnp.split(array, 2, axis=-2), self.orders):
            left = list(live)
            for bit in order:
                part, left = self.halve(part, bit, left)
            parts.append(part)
        return jnp.concatenate(parts, axis=-2)

    def gather(self, array):
        rows, width = array.shape
        parts = []
        for part, order in zip(jnp.split(array, 2, axis=-2), self.orders):
            live = []
            for bit in order[::-1]:
                part, live = self.double(part, bit, live)
            parts.append(part)
        array, _ = self.double(jnp.concatenate(parts, axis=-2), 0, live)
        return array.reshape(self.size, rows, width)


def body(tokens, ln_gain, w_qkv, q_gain, k_gain, w_up, w_out_attn, w_down, cotangent, lengths):
    size = q_gain.shape[0]
    width = tokens.shape[1]
    rows = tokens.shape[0]
    score_scale = 1.0 / math.sqrt(size)
    wide = lax.axis_size("wide")
    images = lengths.shape[0]
    sets = wide // 2
    assert images == sets and wide == 2 * sets
    spot = lax.axis_index("wide")
    group = Group(lax.axis_size("batch"))
    mate = [(w, w ^ 1) for w in range(wide)]

    def shift(by):
        return [(w, (w // 2 + by) % sets * 2 + w % 2) for w in range(wide)]

    token_float = tokens.astype(F32)
    normed, token_inv = normalize(token_float)
    x_own = (normed * ln_gain).astype(LOW)
    x_mate = lax.ppermute(x_own, "wide", mate)
    c_mate = lax.ppermute(cotangent, "wide", mate)
    x = jnp.concatenate([x_own, x_mate], axis=0)
    cot = jnp.concatenate([cotangent, c_mate], axis=0)

    parity = spot % 2
    slots = jnp.arange(rows, dtype=jnp.int32)
    positions = jnp.concatenate([slots + parity * rows, slots + (1 - parity) * rows])
    bias = jnp.where(positions < pick(lengths, spot // 2, 0), 0.0, -1e30).astype(F32)[None]
    gains = jnp.stack([q_gain, k_gain], axis=1)
    fold = jnp.stack([q_gain * (score_scale * LOG2E), k_gain], axis=1)

    w_qkv_t = w_qkv.T
    w_up_t = w_up.T
    packs = [(w_qkv_t, w_out_attn), (w_up_t, w_down)]
    others = range(1, sets)

    def fetch(pack):
        own = [pick(w.reshape(group.size, -1, width), group.index, 0) for w in pack]
        steps = [w.shape[0] for w in own]
        chunk = jnp.concatenate(own, axis=0)
        got = jnp.concatenate([lax.ppermute(chunk, "wide", shift(by)) for by in others], axis=0)
        got = group.gather(got).reshape(group.size, len(others), sum(steps), width)
        cuts, at = [], 0
        for step in steps:
            cut = jnp.swapaxes(got[:, :, at : at + step], 0, 1)
            cuts.append(cut.reshape(-1, width))
            at += step
        return cuts

    def give(pair, count):
        packed = jnp.concatenate(
            [g.astype(LOW).reshape(count, group.size, -1, width) for g in pair], axis=2
        )
        packed = jnp.swapaxes(packed, 0, 1)
        part = group.scatter(packed.reshape(group.size, -1, width))
        return part.reshape(count, -1, width)

    weights = [packs, [fetch(pack) for pack in packs]]

    mate_out = mate_in = own_out = own_in = None
    gain_grad = jnp.zeros((2 * size, 128), F32)
    total = [None, None]

    def add(a, b):
        return b if a is None else a + b

    for turn, ((qkv_t, out_w), (up_t, down_w)) in enumerate(weights):
        q_t, k_t, v_t, rstd = project(x, qkv_t, fold, size)
        g_t = nt(out_w, cot).astype(LOW)
        att_t, raw_t, lanes = attend(q_t, k_t, v_t, g_t, bias, rstd, gains, size, score_scale)
        gain_grad = gain_grad + lanes
        hid_t, gup_t = feed(x, cot, up_t, down_w)
        mate_out = add(mate_out, tn(att_t[:, rows:], out_w) + tn(hid_t[:, rows:], down_w))
        own_out = add(own_out, tn(att_t[:, :rows], out_w) + tn(hid_t[:, :rows], down_w))
        mate_in = add(mate_in, tn(raw_t[:, rows:], qkv_t) + tn(gup_t[:, rows:], up_t))
        own_in = add(own_in, tn(raw_t[:, :rows], qkv_t) + tn(gup_t[:, :rows], up_t))
        grads = [(nn(raw_t, x), nn(att_t, cot)), (nn(gup_t, x), nn(hid_t, cot))]
        for i, pair in enumerate(grads):
            part = give(pair, len(others) if turn else 1)
            if turn:
                parts = [lax.ppermute(part[by - 1], "wide", shift(-by)) for by in others]
            else:
                parts = [part[0]]
            for part in parts:
                total[i] = add(total[i], part.astype(F32))

    branch = own_out + lax.ppermute(mate_out.astype(LOW), "wide", mate).astype(F32)
    output = (token_float + branch).astype(LOW)

    ln_part = jnp.sum(own_in * x_own.astype(F32), axis=0) + jnp.sum(mate_in * x_mate.astype(F32), axis=0)
    small = jnp.concatenate([ln_part / ln_gain, jnp.sum(gain_grad, axis=1)])
    for bit in range(wide.bit_length() - 1):
        small = small + lax.ppermute(small, "wide", [(w, w ^ (1 << bit)) for w in range(wide)])
    for bit in range(group.bits):
        small = small + group.swap(small, bit)

    grad_normed = own_in + lax.ppermute(mate_in.astype(LOW), "wide", mate).astype(F32)
    u = grad_normed * ln_gain
    input_grad = cotangent.astype(F32) + token_inv * (
        u
        - jnp.mean(u, axis=-1, keepdims=True)
        - normed * jnp.mean(u * normed, axis=-1, keepdims=True)
    )

    outs = []
    for part, pack in zip(total, packs):
        whole = group.gather(part.astype(LOW))
        at = 0
        for w in pack:
            step = w.shape[0] // group.size
            outs.append(whole[:, at : at + step].reshape(w.shape).astype(F32))
            at += step
    return (
        output,
        input_grad,
        small[:width],
        outs[0].T,
        small[width : width + size],
        small[width + size :],
        outs[2].T,
        outs[1],
        outs[3],
    )


def solution(mesh):
    placed = (
        P(("batch", "wide"), None),
        P(),
        P(None, "wide"),
        P(),
        P(),
        P(None, "wide"),
        P("wide", None),
        P("wide", None),
        P(("batch", "wide"), None),
        P("batch"),
    )
    return jax.shard_map(
        body,
        mesh=mesh,
        in_specs=placed,
        out_specs=(
            P(("batch", "wide"), None),
            P(("batch", "wide"), None),
            P(),
            P(None, "wide"),
            P(),
            P(),
            P(None, "wide"),
            P("wide", None),
            P("wide", None),
        ),
        check_vma=False,
    )
```

```python
from functools import partial
import math

import jax
import jax.numpy as jnp
from jax import lax
from jax.experimental import pallas as pl
from jax.experimental.pallas import tpu as pltpu
from jax.sharding import PartitionSpec as P


F32 = jnp.float32
LOW = jnp.bfloat16
LOG2E = math.log2(math.e)
LN2 = math.log(2.0)


def nn(a, b):
    return lax.dot_general(a, b, (((1,), (0,)), ((), ())), preferred_element_type=F32)


def nt(a, b):
    return lax.dot_general(a, b, (((1,), (1,)), ((), ())), preferred_element_type=F32)


def tn(a, b):
    return lax.dot_general(a, b, (((0,), (0,)), ((), ())), preferred_element_type=F32)


def normalize(field):
    row_mean = jnp.mean(field, axis=-1, keepdims=True)
    centred = field - row_mean
    variance = jnp.mean(centred * centred, axis=-1, keepdims=True)
    inv = lax.rsqrt(variance + 1e-06)
    return centred * inv, inv


def norm_forward(part):
    centred = part - jnp.mean(part, axis=0, keepdims=True)
    inv = lax.rsqrt(jnp.mean(centred * centred, axis=0, keepdims=True) + 1e-06)
    return centred * inv, inv


def norm_back(grad, scaled, gain, fold, inv):
    n = scaled.astype(F32) * (1.0 / fold)
    u = grad * gain
    back = inv * (
        u - jnp.mean(u, axis=0, keepdims=True) - n * jnp.mean(u * n, axis=0, keepdims=True)
    )
    product = grad * n
    lanes = sum(product[:, c : c + 128] for c in range(0, product.shape[1], 128))
    return back.astype(LOW), lanes


def fold_rows(grad, x_ref):
    product = grad * x_ref[...].astype(F32)
    return jnp.sum(product.reshape(-1, 8, product.shape[1]), axis=0)


def store_grads(core, refs, pieces, steps):
    if len(refs) == 1:
        at = 0
        for piece, step in zip(pieces, steps):
            refs[0][:, at : at + step, :] = piece.reshape(-1, step, piece.shape[-1]).astype(LOW)
            at += step
        return
    at = 0
    for piece, step in zip(pieces, steps):
        for pair in range(piece.shape[0] // (2 * step)):
            first = piece[2 * pair * step : (2 * pair + 1) * step]
            second = piece[(2 * pair + 1) * step : (2 * pair + 2) * step]
            refs[0][pair, at : at + step, :] = jnp.where(core == 0, first, second).astype(LOW)
            refs[1][pair, at : at + step, :] = jnp.where(core == 0, second, first).astype(LOW)
        at += step


def heads_kernel(
    core_ref, xo_ref, xm_ref, co_ref, cm_ref, bias_ref, gains_ref, *refs, size, scale, steps, split, bare
):
    w_refs, refs = refs[: 1 + split], refs[1 + split :]
    grads, refs = refs[: 1 + split], refs[1 + split :]
    ino_ref, inm_ref, outo_ref, outm_ref, ln_ref, lanes_ref, qkv_ref, g_ref, inv_ref, att_ref = refs
    step = pl.program_id(0)
    heads = pl.num_programs(0)
    rows, width = xo_ref.shape
    halves = (slice(0, rows), slice(rows, 2 * rows))
    n_heads = att_ref.shape[0]

    def part_of_weights(lo, hi):
        sides = [ref[:, 0, lo:hi, :] for ref in w_refs]
        if split:
            low = core_ref[0] == 0
            sides = [jnp.where(low, *sides), jnp.where(low, *sides[::-1])]
        return jnp.stack(sides, axis=1).reshape(-1, width)

    @pl.when(step == 0)
    def _():
        qkv_w = part_of_weights(0, steps[0])
        out_w = part_of_weights(steps[0], sum(steps))
        for half, x_ref, c_ref in zip(halves, (xo_ref, xm_ref), (co_ref, cm_ref)):
            raw = nt(qkv_w, x_ref[...])
            grad = nt(out_w, c_ref[...]).astype(LOW)
            for h in range(n_heads):
                at = 3 * size * h
                query, query_inv = norm_forward(raw[at : at + size])
                key, key_inv = norm_forward(raw[at + size : at + 2 * size])
                qkv_ref[h, :size, half] = (query * gains_ref[:, 2:3]).astype(LOW)
                qkv_ref[h, size : 2 * size, half] = (key * gains_ref[:, 1:2]).astype(LOW)
                qkv_ref[h, 2 * size :, half] = raw[at + 2 * size : at + 3 * size].astype(LOW)
                g_ref[h, :, half] = grad[h * size : (h + 1) * size]
                inv_ref[h, 0:1, half] = query_inv
                inv_ref[h, 1:2, half] = key_inv
        lanes_ref[...] = jnp.zeros_like(lanes_ref)

    k_t = qkv_ref[step, size : 2 * size, :]
    v_t = qkv_ref[step, 2 * size :, :]
    k_n = k_t.astype(F32).T.astype(LOW)
    v_n = v_t.astype(F32).T
    v_aug = jnp.concatenate([v_n, jnp.ones(v_n.shape, F32)], axis=1).astype(LOW)
    dk = dv = None
    for half in halves:
        q_t = qkv_ref[step, :size, half]
        q_n = q_t.astype(F32).T.astype(LOW)
        g_n = g_ref[step, :, half].astype(F32).T
        weights = jnp.exp2(nn(q_n, k_t) + bias_ref[...])
        weights_low = weights.astype(LOW)
        summed = nn(weights_low, v_aug)
        inv = 1.0 / summed[:, size : size + 1]
        att = summed[:, :size] * inv
        g_scaled = g_n * inv
        inner = jnp.sum(g_scaled * att, axis=1, keepdims=True)
        dp = nn(g_scaled.astype(LOW), v_t)
        ds = (weights * (dp - inner)).astype(LOW)
        att_ref[step, :, half] = att.T.astype(LOW)
        dv_part = nn(g_scaled.T.astype(LOW), weights_low)
        dk_part = nn(q_t, ds)
        dv = dv_part if dv is None else dv + dv_part
        dk = dk_part if dk is None else dk + dk_part
        dq = nn(ds, k_n).T * scale
        q_back, q_lanes = norm_back(
            dq, q_t, gains_ref[:, 0:1], gains_ref[:, 2:3], inv_ref[step, 0:1, half]
        )
        qkv_ref[step, :size, half] = q_back
        lanes_ref[:size, :] += q_lanes
    k_back, k_lanes = norm_back(
        dk * LN2, k_t, gains_ref[:, 1:2], gains_ref[:, 1:2], inv_ref[step, 1:2, :]
    )
    qkv_ref[step, size : 2 * size, :] = k_back
    qkv_ref[step, 2 * size :, :] = dv.astype(LOW)
    lanes_ref[size:, :] += k_lanes

    @pl.when(step == heads - 1)
    def _():
        qkv_w = part_of_weights(0, steps[0])
        out_w = part_of_weights(steps[0], sum(steps))
        own, mate = halves
        raw_o = qkv_ref[:, :, own].reshape(-1, rows)
        raw_m = qkv_ref[:, :, mate].reshape(-1, rows)
        att_o = att_ref[:, :, own].reshape(-1, rows)
        att_m = att_ref[:, :, mate].reshape(-1, rows)
        g_qkv = nn(raw_o, xo_ref[...]) + nn(raw_m, xm_ref[...])
        g_out = nn(att_o, co_ref[...]) + nn(att_m, cm_ref[...])
        store_grads(core_ref[0], grads, (g_qkv, g_out), steps)
        in_o = tn(raw_o, qkv_w)
        in_m = tn(raw_m, qkv_w)
        ino_ref[...] = in_o.astype(LOW)
        inm_ref[...] = in_m.astype(LOW)
        ln_ref[...] = fold_rows(in_o, xo_ref) + fold_rows(in_m, xm_ref)
        outo_ref[...] = tn(att_o, out_w).astype(LOW)
        outm_ref[...] = att_m if bare else tn(att_m, out_w).astype(LOW)


def side_specs(arrays, natural, block, at):
    def index(side):
        def of(i, core):
            place = i if at is not None else 0
            chosen = 0 if not natural else core[0] if side == 0 else 1 - core[0]
            return (place, chosen, at or 0, 0)

        return of

    return [pl.BlockSpec((block[0], 1, *block[1:]), index(side)) for side in range(len(arrays))]


def heads_call(core, x, cot, pack, bias, gains, size, scale, bare=False):
    rows, width = x[0].shape
    arrays, natural, steps = pack
    split = len(arrays) - 1
    places = arrays[0].shape[0]
    heads = places * len(arrays) * steps[1] // size
    one = lambda *dims: pl.BlockSpec(dims, lambda h, core: (0,) * len(dims))
    grad = one(places, sum(steps), width)
    grad_out = jax.ShapeDtypeStruct((places, sum(steps), width), LOW)
    act = one(rows, width)
    low = jax.ShapeDtypeStruct((rows, width), LOW)
    last = (heads * size, rows) if bare else (rows, width)
    return pl.pallas_call(
        partial(heads_kernel, size=size, scale=scale, steps=steps, split=split, bare=bare),
        grid_spec=pltpu.PrefetchScalarGridSpec(
            num_scalar_prefetch=1,
            grid=(heads,),
            in_specs=[act, act, act, act, one(1, 2 * rows), one(size, 3)]
            + side_specs(arrays, natural, (places, sum(steps), width), None),
            out_specs=[grad] * (1 + split) + [act, act, act, one(*last), one(8, width), one(2 * size, 128)],
            scratch_shapes=[
                pltpu.VMEM((heads, 3 * size, 2 * rows), LOW),
                pltpu.VMEM((heads, size, 2 * rows), LOW),
                pltpu.VMEM((heads, 2, 2 * rows), F32),
                pltpu.VMEM((heads, size, 2 * rows), LOW),
            ],
        ),
        out_shape=[grad_out] * (1 + split)
        + [
            low,
            low,
            low,
            jax.ShapeDtypeStruct(last, LOW),
            jax.ShapeDtypeStruct((8, width), F32),
            jax.ShapeDtypeStruct((2 * size, 128), F32),
        ],
        compiler_params=pltpu.CompilerParams(vmem_limit_bytes=60 << 20),
        name="heads",
    )(core, *x, *cot, bias, gains, *arrays)


def feed_kernel(core_ref, *refs, count, sides, prior):
    def take(number):
        nonlocal refs
        taken, refs = refs[:number], refs[number:]
        return taken

    x_refs, c_refs, up_refs, down_refs = take(count), take(count), take(sides), take(sides)
    prior_refs = take(sides if prior else 0)
    grads, in_refs, out_refs = take(sides), take(count), take(count)
    ln_ref, accin_ref, accout_ref = refs
    width = accin_ref.shape[2]
    step_up = up_refs[0].shape[2]
    up_w = jnp.concatenate([r[...].reshape(-1, width) for r in up_refs], axis=0)
    down_w = jnp.concatenate([r[...].reshape(-1, width) for r in down_refs], axis=0)
    g_up = g_down = None
    if prior:
        g_up = jnp.concatenate([r[:, :step_up].reshape(-1, width) for r in prior_refs], axis=0).astype(F32)
        g_down = jnp.concatenate([r[:, step_up:].reshape(-1, width) for r in prior_refs], axis=0).astype(F32)

    @pl.when(pl.program_id(0) == 0)
    def _():
        accin_ref[...] = jnp.zeros_like(accin_ref)
        accout_ref[...] = jnp.zeros_like(accout_ref)

    for i in range(count):
        x = x_refs[i][...]
        cot = c_refs[i][...]
        up = nt(up_w, x)
        grad_hidden = nt(down_w, cot)
        half = 0.5 + 0.5 * lax.erf(up * math.sqrt(0.5))
        bell = jnp.exp(up * up * -0.5) * (1.0 / math.sqrt(2.0 * math.pi))
        hidden = (up * half).astype(LOW)
        grad = (grad_hidden * (half + up * bell)).astype(LOW)
        up_part = nn(grad, x)
        down_part = nn(hidden, cot)
        g_up = up_part if g_up is None else g_up + up_part
        g_down = down_part if g_down is None else g_down + down_part
        accin_ref[i] += tn(grad, up_w)
        accout_ref[i] += tn(hidden, down_w)
    for i, ref in enumerate(grads):
        for at, value in ((0, g_up), (step_up, g_down)):
            own = value.shape[0] // sides
            part = value[i * own : (i + 1) * own].astype(LOW).reshape(ref.shape[0], -1, width)
            ref[:, at : at + part.shape[1], :] = part

    @pl.when(pl.program_id(0) == pl.num_programs(0) - 1)
    def _():
        for i in range(count):
            in_refs[i][...] = accin_ref[i].astype(LOW)
            out_refs[i][...] = accout_ref[i].astype(LOW)
        ln_ref[...] = sum(fold_rows(accin_ref[i], x_refs[i]) for i in range(count))


def feed_call(core, x, cot, up, down, prior=()):
    rows, width = x[0].shape
    count = len(x)
    arrays, natural, up_at, up_step = up
    downs, _, down_at, down_step = down
    sides = len(arrays)
    places = arrays[0].shape[0]
    per = max(1, min(places, 512 // (up_step * sides)))
    act = pl.BlockSpec((rows, width), lambda i, core: (0, 0))
    low = jax.ShapeDtypeStruct((rows, width), LOW)
    both = up_step + down_step
    grad = pl.BlockSpec((per, both, width), lambda i, core: (i, 0, 0))
    return pl.pallas_call(
        partial(feed_kernel, count=count, sides=sides, prior=bool(prior)),
        grid_spec=pltpu.PrefetchScalarGridSpec(
            num_scalar_prefetch=1,
            grid=(places // per,),
            in_specs=[act] * (2 * count)
            + side_specs(arrays, natural, (per, up_step, width), up_at)
            + side_specs(downs, natural, (per, down_step, width), down_at)
            + [grad] * len(prior),
            out_specs=[grad] * sides
            + [act] * (2 * count)
            + [pl.BlockSpec((8, width), lambda i, core: (0, 0))],
            scratch_shapes=[pltpu.VMEM((count, rows, width), F32)] * 2,
        ),
        out_shape=[jax.ShapeDtypeStruct((places, both, width), LOW)] * sides
        + [low] * (2 * count)
        + [jax.ShapeDtypeStruct((8, width), F32)],
        compiler_params=pltpu.CompilerParams(vmem_limit_bytes=60 << 20),
        name="feed",
    )(core, *x, *cot, *arrays, *downs, *prior)


def place_kernel(spot_ref, *refs, count, steps):
    near, far, (turned_ref, plain_ref) = refs[:count], refs[count : 2 * count], refs[2 * count :]
    low = spot_ref[1] == 0
    chunks = []
    for a, b in zip(near, far):
        mine, theirs = a[0].astype(F32), b[0].astype(F32)
        chunks += [jnp.where(low, mine, theirs), jnp.where(low, theirs, mine)]
    turned_ref[...] = jnp.concatenate([c[: steps[0]] for c in chunks], axis=0).T
    plain_ref[...] = jnp.concatenate([c[steps[0] :] for c in chunks], axis=0)


def place(spot, near, far, steps, count):
    half, rows, width = near.shape
    block = lambda p: pl.BlockSpec((1, rows, width), lambda i, spot: ((i * count + p) ^ spot[0], 0, 0))
    blocks = [block(p) for p in range(count)]
    turned, plain = (2 * count * step for step in steps)
    return pl.pallas_call(
        partial(place_kernel, count=count, steps=steps),
        grid_spec=pltpu.PrefetchScalarGridSpec(
            num_scalar_prefetch=1,
            grid=(half // count,),
            in_specs=blocks + blocks,
            out_specs=[
                pl.BlockSpec((width, turned), lambda i, spot: (0, i)),
                pl.BlockSpec((plain, width), lambda i, spot: (i, 0)),
            ],
        ),
        out_shape=[
            jax.ShapeDtypeStruct((width, 2 * half * steps[0]), F32),
            jax.ShapeDtypeStruct((2 * half * steps[1], width), F32),
        ],
        name="place",
    )(spot, *[near] * count, *[far] * count)


def pick(array, index, axis=0):
    return lax.dynamic_index_in_dim(array, index, axis, keepdims=False)


def after(value, *others):
    return lax.optimization_barrier((value, *others))[0]


class Group:
    def __init__(self, size):
        self.size = size
        self.half = size // 2
        self.index = lax.axis_index("batch")
        self.core = self.index % 2
        self.rest = self.index // 2

    def send(self, array, distance):
        return lax.ppermute(array, "batch", [(b, b ^ distance) for b in range(self.size)])

    def reduce(self, kept, sent, natural):
        got = self.send(sent, 1)
        parts = []
        for m in range(self.half):
            place = self.rest ^ m if natural else m
            parts.append(pick(kept, place).astype(F32) + pick(got, place).astype(F32))
        total = parts[0]
        others = [self.send(parts[m].astype(LOW), 2 * m) for m in range(1, self.half)]
        for other in others:
            total = total + other.astype(F32)
        return total

    def gather(self, array):
        others = [self.send(array, 2 * m) for m in range(1, self.half)]
        near = jnp.stack([array] + others)
        return near, self.send(near, 1)

    def straight(self, near, far):
        order = jnp.arange(self.half, dtype=jnp.int32) ^ self.rest
        low = self.core == 0
        both = jnp.stack([jnp.where(low, near, far), jnp.where(low, far, near)], axis=1)
        return jnp.take(both, order, axis=0).reshape(self.size, *near.shape[1:])


def compute(tokens, ln_gain, w_qkv, q_gain, k_gain, w_up, w_out_attn, w_down, cotangent, lengths):
    size = q_gain.shape[0]
    rows, width = tokens.shape
    scale = 1.0 / math.sqrt(size)
    wide = lax.axis_size("wide")
    sets = wide // 2
    assert lengths.shape[0] == sets and wide == 2 * sets
    spot = lax.axis_index("wide")
    group = Group(lax.axis_size("batch"))
    mate = [(w, w ^ 1) for w in range(wide)]
    heads_steps = (w_qkv.shape[1] // group.size, w_out_attn.shape[0] // group.size)
    feed_steps = (w_up.shape[1] // group.size, w_down.shape[0] // group.size)
    split = int(heads_steps[0] % 16 == 0 and heads_steps[1] % 16 == 0)

    def shift(by):
        return [(w, (w // 2 + by) % sets * 2 + w % 2) for w in range(wide)]

    def swap(array):
        return lax.ppermute(array, "wide", mate)

    token_float = tokens.astype(F32)
    normed, token_inv = normalize(token_float)
    x_o = (normed * ln_gain).astype(LOW)
    x_m = swap(x_o)

    def chunk_of(w, axis):
        step = w.shape[axis] // group.size
        part = lax.dynamic_slice_in_dim(w, group.index * step, step, axis)
        return part.T if axis else part

    feed_chunk = jnp.concatenate([chunk_of(w_up, 1), chunk_of(w_down, 0)])
    heads_chunk = jnp.concatenate([chunk_of(w_qkv, 1), chunk_of(w_out_attn, 0)])
    fetched_feed = [lax.ppermute(feed_chunk, "wide", shift(by)) for by in range(1, sets)]
    c_o = cotangent
    c_m = swap(c_o)
    heads_chunk = after(heads_chunk, c_m)
    fetched_heads = [lax.ppermute(heads_chunk, "wide", shift(by)) for by in range(1, sets)]

    parity = spot % 2
    slots = jnp.arange(rows, dtype=jnp.int32)
    positions = jnp.concatenate([slots + parity * rows, slots + (1 - parity) * rows])
    bias = jnp.where(positions < pick(lengths, spot // 2), 0.0, -1e30).astype(F32)[None]
    gains = jnp.stack([q_gain, k_gain, q_gain * (scale * LOG2E)], axis=1)
    core = group.core.reshape(1)

    def heads_of(qkv_t, out_w):
        if split:
            parts = [w.reshape(group.half, 2, -1, width) for w in (qkv_t, out_w)]
            pack = jnp.concatenate(parts, axis=2)
            return (pack, pack), True, heads_steps
        count = out_w.shape[0] // size
        pack = jnp.concatenate([w.reshape(count, 1, -1, width) for w in (qkv_t, out_w)], axis=2)
        return (pack,), False, (3 * size, size)

    def feed_of(up_t, down_w):
        if split:
            views = [w.reshape(group.half, 2, -1, width) for w in (up_t, down_w)]
            return [((v, v), True, 0, step) for v, step in zip(views, feed_steps)]
        return [((w[None, None],), False, 0, w.shape[0]) for w in (up_t, down_w)]

    def cut(near, far, steps):
        got = group.straight(near, far)
        return [got[:, : steps[0]].reshape(-1, width), got[:, steps[0] :].reshape(-1, width)]

    def far_feed(got):
        near, far = group.gather(got)
        if split:
            sides = (near[:, None], far[:, None])
            return [(sides, False, at, step) for at, step in enumerate(feed_steps)]
        return feed_of(*cut(near, far, feed_steps))

    def far_heads(got):
        near, far = group.gather(got)
        if split:
            return (near[:, None], far[:, None]), False, heads_steps
        return heads_of(*cut(near, far, heads_steps))

    def reduced(grads, whole, natural):
        if split:
            return group.reduce(*grads, natural)
        parts, at = [], 0
        for step in whole:
            parts.append(grads[0][:, at : at + step].reshape(group.size, -1, width))
            at += step
        packed = jnp.concatenate(parts, axis=1).reshape(group.half, 2, -1, width)
        return group.reduce(pick(packed, group.core, 1), pick(packed, 1 - group.core, 1), True)

    heads_whole = (3 * size, size)
    feed_whole = (w_up.shape[1], w_down.shape[0])
    sides = 1 + split

    own_heads = heads_of(w_qkv.T, w_out_attn)
    own_feed = feed_of(w_up.T, w_down)
    first = feed_call(core, [x_o], [c_o], *own_feed)
    in_a, out_a, ln_a = first[sides:]
    feeds = [far_feed(after(got, in_a)) for got in fetched_feed]
    heads = [far_heads(after(got, in_a)) for got in fetched_heads]
    x_m, bias, gains, *packs = lax.optimization_barrier((x_m, bias, gains, *own_heads[0]))
    own_heads = (tuple(packs), *own_heads[1:])
    second = feed_call(core, [x_m], [c_m], *own_feed, first[:sides])
    in_b, out_b, ln_b = second[sides:]
    feed_sum = reduced(second[:sides], feed_whole, True)

    in_own, in_mate, out_own, out_mate = [in_a], [in_b], [out_a], [out_b]

    ln_parts = [ln_a, ln_b]

    def run(results):
        grads, (io, im, oo, om) = results[:sides], results[sides : sides + 4]
        in_own.append(io), in_mate.append(im), out_own.append(oo), out_mate.append(om)
        ln_parts.append(results[sides + 4])
        return grads, im, results[sides + 5 :]

    def home(part, by):
        return lax.ppermute(part.astype(LOW), "wide", shift(-by)).astype(F32)

    x = [x_o, x_m]
    heads_sum, lanes, last = None, None, in_b
    out_w_mate = swap(after(w_out_attn, in_b))
    for by in range(1, sets):
        cot = [c_o, after(c_m, last)]
        grads, last, _ = run(feed_call(core, x, cot, *feeds[by - 1]))
        feed_sum = feed_sum + home(reduced(grads, feed_whole, False), by)
        cot = [c_o, after(c_m, last)]
        grads, last, (more,) = run(
            heads_call(core, x, cot, heads[by - 1], bias, gains, size, scale)
        )
        part = home(reduced(grads, heads_whole, False), by)
        heads_sum = part if heads_sum is None else heads_sum + part
        lanes = more if lanes is None else lanes + more

    def total(parts):
        result = parts[0].astype(F32)
        for part in parts[1:]:
            result = result + part.astype(F32)
        return result

    out_got = swap(total(out_mate).astype(LOW))
    cot = [c_o, after(c_m, last)]
    grads, last, (more,) = run(
        heads_call(core, x, cot, own_heads, bias, gains, size, scale, bare=True)
    )
    att_got = swap(out_mate[-1])
    heads_sum = heads_sum + reduced(grads, heads_whole, True)
    lanes = lanes + more

    in_got = swap(total(in_mate).astype(LOW))
    in_own_sum = total(in_own)
    ln_part = jnp.sum(total(ln_parts), axis=0)
    small = jnp.concatenate([ln_part / ln_gain, jnp.sum(lanes, axis=1)])
    for bit in range(wide.bit_length() - 1):
        small = small + lax.ppermute(small, "wide", [(w, w ^ (1 << bit)) for w in range(wide)])
    for bit in range(group.size.bit_length() - 1):
        small = small + group.send(small, 1 << bit)

    def results(chunk_sum, steps, count):
        near, far = group.gather(chunk_sum.astype(LOW))
        if split:
            return place(jnp.stack([group.rest, group.core]), near, far, steps, count)
        both = group.straight(near, far).astype(F32)
        first = both[:, : steps[0]].reshape(-1, width).T
        return first, both[:, steps[0] :].reshape(-1, width)

    g_up, g_down = results(feed_sum, feed_steps, 1)
    g_qkv, g_out = results(heads_sum, heads_steps, 2)

    from_mate = out_got.astype(F32) + tn(att_got, out_w_mate)
    output = (token_float + total(out_own) + from_mate).astype(LOW)
    u = (in_own_sum + in_got.astype(F32)) * ln_gain
    input_grad = cotangent.astype(F32) + token_inv * (
        u
        - jnp.mean(u, axis=-1, keepdims=True)
        - normed * jnp.mean(u * normed, axis=-1, keepdims=True)
    )
    return (
        output,
        input_grad,
        small[:width],
        g_qkv,
        small[width : width + size],
        small[width + size :],
        g_up,
        g_out,
        g_down,
    )


def solution(mesh):
    placed = (
        P(("batch", "wide"), None),
        P(),
        P(None, "wide"),
        P(),
        P(),
        P(None, "wide"),
        P("wide", None),
        P("wide", None),
        P(("batch", "wide"), None),
        P("batch"),
    )
    return jax.shard_map(
        compute,
        mesh=mesh,
        in_specs=placed,
        out_specs=(
            P(("batch", "wide"), None),
            P(("batch", "wide"), None),
            P(),
            P(None, "wide"),
            P(),
            P(),
            P(None, "wide"),
            P("wide", None),
            P("wide", None),
        ),
        check_vma=False,
    )
```
